256 devices in a mesh: ta: 32 (over x, y, core), ka: 8 (over z).
Axes of the slice: x: 4, y: 4, z: 8, core: 2. Of those that a mesh axis runs over, the one named last changes fastest.
Arguments:
- amplitudes: bfloat16 [512, 163840], P('ka', 'ta'), may hold values from -6 to 6
- integrals: bfloat16 [163840, 5120], P('ta', 'ka'), may hold values from -0.1875 to 0.1875
- other_terms: bfloat16 [512, 163840], P('ka', 'ta'), may hold values from -6 to 6
- tile_block: int32 [1280], replicated, may hold values from 0 to 1279, as said below
- occ_pairs: int32 [512, 2], P('ka'), may hold values from 0 to 149
- occ_energy: float32 [150], replicated, may hold values from -2 to -0.3
- pair_energy: float32 [163840], P('ta'), may hold values from 0.4 to 6
Outputs:
- increment: float32 [512, 163840], P('ka', 'ta')
The draws below stay inside these ranges and needn't reach their ends.
Inputs may be any that keep to these rules, and one draw needn't show every extreme that they name: `tile_block`: the tiles of one symmetry block share one id, the index of the block's last tile, so ids never fall from tile to tile; a block lies within one region of 40 tiles, spans at most 16 tiles, and every region holds exactly one block of 16 tiles.
All inputs are finite; a program needn't handle non-finite values.
Results may differ from the reference program's by a relative error of at most 0.0075.
Values may be sent and summed in bfloat16 or wider, within the bound.
No kernel may reach another device: no remote copies, remote signals or barrier semaphores. Data moves between devices by JAX's collectives and lax.ppermute only.
A program may use at most 128 MiB of HBM per device.

```python
import jax
import jax.numpy as jnp
from jax import lax

NOCC = 150
OPAIRS = 512
REG = 5120
TILE = 128
MAXBT = 16
P_SIZE = 163840
NTILE = 1280
RTILE = 40
N_TA = 32
N_KA = 8


def draw_tile_block(key, part):
    regions = NTILE // RTILE
    first_key, second_key, third_key = jax.random.split(jax.random.fold_in(key, 11), 3)
    start = jax.random.randint(first_key, (regions, 1), 0, RTILE - MAXBT + 1)
    offset = jax.random.randint(third_key, (regions, 1), 0, MAXBT - 1)
    position = jnp.arange(RTILE, dtype=jnp.int32)[None, :]
    coin = jax.random.randint(second_key, (regions, RTILE), 0, 6) == 0
    forced = (position - offset) % (MAXBT - 1) == 0
    inside = (position > start) & (position < start + MAXBT)
    edge = (position == 0) | (position == start) | (position == start + MAXBT) | forced | coin
    flags = jnp.where(edge & jnp.logical_not(inside), 1, 0).astype(jnp.int32).reshape(-1)
    following = jnp.concatenate([flags[1:], jnp.ones((1,), jnp.int32)])
    tile_index = jnp.arange(NTILE, dtype=jnp.int32)
    block_ends = jnp.where(following == 1, tile_index, NTILE).astype(jnp.int32)
    return lax.cummin(block_ends, axis=0, reverse=True).astype(jnp.int32)


def with_ends(values, rng, low, high):
    longest = values.shape.index(max(values.shape))
    spots = []
    for shift in (0, 1):
        where = [jax.random.randint(jax.random.fold_in(rng, axis), (), 0, length) for axis, length in enumerate(values.shape)]
        where[longest] = (where[longest] + shift) % values.shape[longest]
        spots.append(tuple(where))
    return values.at[spots[0]].set(low).at[spots[1]].set(high)


def levels(stream_key, extent, cuts, smallest, top_value):
    level = 1.0
    for axis_at, shards_of in cuts:
        draws = jax.random.uniform(jax.random.fold_in(jax.random.fold_in(stream_key, 6), axis_at), (shards_of,), jnp.float32, smallest / len(cuts), top_value / len(cuts))
        level = level * jnp.repeat(jnp.exp(draws), extent[axis_at] // shards_of).reshape((-1,) + (1,) * (len(extent) - 1 - axis_at))
    return level


def normal_values(stream_key, extent, scale, most, shards=(), held_as=jnp.bfloat16):
    values = scale * jax.random.normal(stream_key, extent, jnp.float32)
    if shards:
        values = values * levels(stream_key, extent, shards, -0.22, 0.18)
    return jnp.clip(values, -most, most).astype(held_as)


def setup_inputs(seed: int = 0) -> dict:
    splits = jax.random.split(jax.random.key(seed), 8)
    amplitudes = normal_values(splits[0], (OPAIRS, P_SIZE), 1.0, 6.0, ((0, 8), (1, 32)))
    integrals = normal_values(splits[1], (P_SIZE, REG), 1024 ** -0.5, 0.1875, ((0, 32), (1, 8)))
    other_terms = normal_values(splits[2], (OPAIRS, P_SIZE), 1.0, 6.0, ((0, 8), (1, 32)))
    tile_block = draw_tile_block(jax.random.fold_in(splits[7], 71), 0)
    occ_pairs = with_ends(jax.random.randint(splits[4], (OPAIRS, 2), 0, NOCC), jax.random.fold_in(splits[4], 1), 0, NOCC - 1).astype(jnp.int32)
    occ_energy = jnp.clip(jax.random.uniform(splits[5], (NOCC,), jnp.float32, -2.0, -0.3), -2.0, -0.3)
    pair_energy = jnp.clip(0.4 + 5.6 * jax.random.uniform(splits[6], (P_SIZE,), jnp.float32) ** levels(splits[6], (P_SIZE,), ((0, 32),), -0.2, 0.2), 0.4, 6.0)
    return dict(amplitudes=amplitudes, integrals=integrals, other_terms=other_terms, tile_block=tile_block, occ_pairs=occ_pairs, occ_energy=occ_energy, pair_energy=pair_energy)


def reference(amplitudes, integrals, other_terms, tile_block, occ_pairs, occ_energy, pair_energy):
    slice_rows = REG // N_TA
    stripe = REG // N_KA
    dealt = integrals.reshape(N_TA, N_TA, slice_rows, REG)
    regional = amplitudes.reshape(OPAIRS, N_TA, REG)
    region_tiles = tile_block.reshape(N_TA, RTILE)

    def one_region(index):
        block_rows = lax.dynamic_index_in_dim(dealt, index, axis=1, keepdims=False).reshape(REG, REG)
        tiles = lax.dynamic_index_in_dim(region_tiles, index, axis=0, keepdims=False)
        pair_blocks = jnp.repeat(tiles, TILE)
        matches = pair_blocks[:, None] == pair_blocks[None, :]
        kept = jnp.where(matches, block_rows, jnp.zeros((), block_rows.dtype)).astype(jnp.float32)
        factor = lax.dynamic_index_in_dim(regional, index, axis=1, keepdims=False).astype(jnp.float32)
        total = jnp.zeros((OPAIRS, REG), jnp.float32)
        for part in range(N_KA):
            term = jnp.dot(factor[:, part * stripe:(part + 1) * stripe], kept[:, part * stripe:(part + 1) * stripe].T, precision=lax.Precision.HIGHEST)
            term = lax.optimization_barrier(term.astype(jnp.bfloat16)).astype(jnp.float32)
            total = total + term
        return total

    ladder = lax.map(one_region, jnp.arange(N_TA, dtype=jnp.int32))
    ladder = jnp.transpose(ladder, (1, 0, 2)).reshape(OPAIRS, N_TA * REG)
    occupied_sum = occ_energy[occ_pairs[:, 0]] + occ_energy[occ_pairs[:, 1]]
    denominator = occupied_sum[:, None] - pair_energy[None, :]
    residual = other_terms.astype(jnp.float32) + ladder
    return residual / denominator
```

```python
import jax
import jax.numpy as jnp
from jax import lax
from jax.experimental import pallas as pl
from jax.experimental.pallas import tpu as pltpu
from jax.sharding import PartitionSpec as P

TILE = 128
UNIT = 32
STEP = 512


def block_of(tiles, index):
    picker = (index[:, None] == jnp.arange(tiles.shape[0], dtype=jnp.int32)[None, :]).astype(jnp.float32)
    return jnp.dot(picker, tiles, precision=lax.Precision.HIGHEST)


def gather_kernel(index_ref, *refs):
    stripes, window_ref = refs[:-1], refs[-1]
    rows = stripes[0].shape[0]
    for step, stripe in enumerate(stripes):
        slot = lax.rem(index_ref[0] + step, len(stripes))
        window_ref[pl.ds(pl.multiple_of(slot * rows, rows), rows), :] = stripe[...]


def gather(index, stripes):
    rows, width = stripes[0].shape
    return pl.pallas_call(
        gather_kernel,
        in_specs=[pl.BlockSpec(memory_space=pltpu.SMEM)] + [pl.BlockSpec(memory_space=pltpu.VMEM)] * len(stripes),
        out_specs=pl.BlockSpec(memory_space=pltpu.VMEM),
        out_shape=jax.ShapeDtypeStruct((rows * len(stripes), width), stripes[0].dtype),
        name="gather_window",
    )(index, *stripes)


def product_kernel(keep_ref, window_ref, rows_ref, out_ref, masked_ref):
    for unit in range(masked_ref.shape[0] // UNIT):
        rows = pl.ds(unit * UNIT, UNIT)
        keep = keep_ref[unit : unit + 1, :].astype(jnp.bfloat16)
        masked_ref[rows, :] = rows_ref[rows, :] * keep
    out_ref[...] = lax.dot_general(
        window_ref[...], masked_ref[...], (((1,), (1,)), ((), ())), preferred_element_type=jnp.float32
    ).astype(jnp.bfloat16)


def product(window, rows, keep):
    occ, stripe = window.shape
    count = rows.shape[0]
    return pl.pallas_call(
        product_kernel,
        grid=(count // STEP,),
        in_specs=[
            pl.BlockSpec((STEP // UNIT, stripe), lambda t: (t, 0)),
            pl.BlockSpec((occ, stripe), lambda t: (0, 0)),
            pl.BlockSpec((STEP, stripe), lambda t: (t, 0)),
        ],
        out_specs=pl.BlockSpec((occ, STEP), lambda t: (0, t)),
        out_shape=pltpu.HBM((occ, count), jnp.bfloat16),
        scratch_shapes=[pltpu.VMEM((STEP, stripe), jnp.bfloat16)],
        compiler_params=pltpu.CompilerParams(vmem_limit_bytes=16 * 1024 * 1024),
        cost_estimate=pl.CostEstimate(
            flops=2 * occ * stripe * count,
            bytes_accessed=2 * (occ * stripe + count * stripe + occ * count),
            transcendentals=0,
        ),
        name="product",
    )(keep, window, rows)


def shards(amplitudes, integrals, other_terms, tile_block, occ_pairs, occ_energy, pair_energy):
    wide_count = lax.axis_size("ta")
    wide_index = lax.axis_index("ta")
    narrow_count = lax.axis_size("ka")
    narrow_index = lax.axis_index("ka")
    region, stripe = integrals.shape
    slice_rows = region // wide_count
    region_tiles = region // TILE

    stripes = []
    for step in range(narrow_count):
        column = lax.rem(narrow_index + narrow_count - step, narrow_count) * stripe
        part = lax.dynamic_slice(amplitudes, (0, column), (amplitudes.shape[0], stripe))
        pairs = [(i, (i + narrow_count - step) % narrow_count) for i in range(narrow_count)]
        stripes.append(lax.ppermute(part, "ka", pairs) if step else part)
    window = gather(narrow_index.reshape(1), stripes)

    arrived = lax.all_to_all(
        integrals.reshape(wide_count, slice_rows, stripe), "ta", split_axis=0, concat_axis=0, tiled=True
    ).reshape(region, stripe)

    tiles = lax.dynamic_slice(tile_block, (wide_index * region_tiles,), (region_tiles,)).astype(jnp.float32)
    columns = (narrow_index * stripe + jnp.arange(stripe, dtype=jnp.int32)) // TILE
    units = jnp.arange(region // UNIT, dtype=jnp.int32) * UNIT // TILE
    keep = (block_of(tiles, units)[:, None] == block_of(tiles, columns)[None, :]).astype(jnp.float32)

    occ_count = occ_energy.shape[0]
    choosers = (
        occ_pairs.reshape(-1)[:, None] == jnp.arange(occ_count, dtype=jnp.int32)[None, :]
    ).astype(jnp.float32)
    energies = jnp.dot(choosers, occ_energy, precision=lax.Precision.HIGHEST).reshape(occ_pairs.shape[0], 2)
    occupied_sum = energies[:, 0] + energies[:, 1]
    denominator = occupied_sum[:, None] - pair_energy[None, :]

    shares = product(window, arrived, keep)
    ladder = lax.psum_scatter(shares, "ka", scatter_dimension=0, tiled=True).astype(jnp.float32)
    residual = other_terms.astype(jnp.float32) + ladder
    return residual / denominator


def solution(mesh):
    return jax.shard_map(
        shards,
        mesh=mesh,
        in_specs=(P("ka", "ta"), P("ta", "ka"), P("ka", "ta"), P(), P("ka", None), P(), P("ta")),
        out_specs=P("ka", "ta"),
        check_vma=False,
    )
```

```python
import jax
import jax.numpy as jnp
from jax import lax
from jax.experimental import pallas as pl
from jax.experimental.pallas import tpu as pltpu
from jax.sharding import PartitionSpec as P

TILE = 128
UNIT = 16
COST = pl.CostEstimate(flops=1000, bytes_accessed=1000, transcendentals=0)
CHUNKS = (112, 48)
STEPS = (896, 768)
SPAN = 1280


def block_of(tiles, index):
    picker = (index[:, None] == jnp.arange(tiles.shape[0], dtype=jnp.int32)[None, :]).astype(jnp.float32)
    return jnp.dot(picker, tiles, precision=lax.Precision.HIGHEST)


def gather(stripes, held):
    count = len(stripes)
    rows, width = stripes[0].shape

    def kernel(*refs):
        window_ref = refs[count + len(held)]
        for slot, stripe in enumerate(refs[:count]):
            window_ref[slot * rows : (slot + 1) * rows, :] = stripe[...]

    vmem, anywhere = pl.BlockSpec(memory_space=pltpu.VMEM), pl.BlockSpec(memory_space=pl.ANY)
    window, *held = pl.pallas_call(
        kernel,
        in_specs=[vmem] * count + [anywhere] * len(held),
        out_specs=[vmem] + [anywhere] * len(held),
        out_shape=[jax.ShapeDtypeStruct((rows * count, width), stripes[0].dtype)]
        + [pltpu.HBM(h.shape, h.dtype) for h in held],
        input_output_aliases={count + n: 1 + n for n in range(len(held))},
        name="gather_window",
    )(*stripes, *held)
    return window, held


def product_kernel(keep_ref, window_ref, rows_ref, *refs):
    outs, masked_ref = refs[:-1], refs[-1]
    window = outs[0].shape[0]
    for unit in range(masked_ref.shape[0] // UNIT):
        rows = pl.ds(unit * UNIT, UNIT)
        keep = keep_ref[unit : unit + 1, :].astype(jnp.bfloat16)
        masked_ref[rows, :] = rows_ref[rows, :] * keep
    shares = lax.dot_general(
        window_ref[...], masked_ref[...], (((1,), (1,)), ((), ())), preferred_element_type=jnp.float32
    ).astype(jnp.bfloat16)
    for slot, out in enumerate(outs):
        out[...] = shares[slot * window : (slot + 1) * window]


def product(window, rows, keep, slots, step):
    occ, stripe = window.shape
    count = rows.shape[0]
    return pl.pallas_call(
        product_kernel,
        grid=(count // step,),
        in_specs=[
            pl.BlockSpec((step // UNIT, stripe), lambda t: (t, 0)),
            pl.BlockSpec((occ, stripe), lambda t: (0, 0)),
            pl.BlockSpec((step, stripe), lambda t: (t, 0)),
        ],
        out_specs=[pl.BlockSpec((occ // slots, step), lambda t: (0, t))] * slots,
        out_shape=[pltpu.HBM((occ // slots, count), jnp.bfloat16)] * slots,
        scratch_shapes=[pltpu.VMEM((step, stripe), jnp.bfloat16)],
        compiler_params=pltpu.CompilerParams(vmem_limit_bytes=24 * 1024 * 1024),
        cost_estimate=COST,
        name="product",
    )(keep, window, rows)


def finish_kernel(*refs):
    count = len(CHUNKS)
    pieces, places = refs[: 3 * count], refs[3 * count : 4 * count]
    other_ref, occ_ref, pair_ref, out_ref = refs[4 * count :]
    residual = other_ref[...].astype(jnp.float32)
    for chunk, place in enumerate(places):
        own, up, down = (piece[...].astype(jnp.float32) for piece in pieces[3 * chunk : 3 * chunk + 3])
        share = own + up + down
        high = share.astype(jnp.bfloat16)
        low = (share - high.astype(jnp.float32)).astype(jnp.bfloat16)
        residual = residual + jnp.dot(high, place[...], preferred_element_type=jnp.float32)
        residual = residual + jnp.dot(low, place[...], preferred_element_type=jnp.float32)
    out_ref[...] = residual / (occ_ref[...] - pair_ref[...])


def finish(pieces, places, other_terms, occupied_sum, pair_energy):
    window, region = other_terms.shape
    spans = region // SPAN
    return pl.pallas_call(
        finish_kernel,
        grid=(spans,),
        in_specs=[pl.BlockSpec((window, p.shape[1] // spans), lambda t: (0, t)) for p in pieces]
        + [pl.BlockSpec(p.shape, lambda t: (0, 0)) for p in places]
        + [
            pl.BlockSpec((window, SPAN), lambda t: (0, t)),
            pl.BlockSpec((window, 1), lambda t: (0, 0)),
            pl.BlockSpec((1, SPAN), lambda t: (0, t)),
        ],
        out_specs=pl.BlockSpec((window, SPAN), lambda t: (0, t)),
        out_shape=jax.ShapeDtypeStruct((window, region), jnp.float32),
        compiler_params=pltpu.CompilerParams(vmem_limit_bytes=24 * 1024 * 1024),
        cost_estimate=COST,
        name="finish",
    )(*pieces, *places, other_terms, occupied_sum, pair_energy)


def shift(values, count, step):
    return lax.ppermute(values, "ka", [(i, (i + step) % count) for i in range(count)])


def shards(amplitudes, integrals, other_terms, tile_block, occ_pairs, occ_energy, pair_energy):
    wide_count = lax.axis_size("ta")
    wide_index = lax.axis_index("ta")
    narrow_count = lax.axis_size("ka")
    narrow_index = lax.axis_index("ka")
    region, stripe = integrals.shape
    slice_rows = region // wide_count
    region_tiles = region // TILE
    dealt = integrals.reshape(wide_count, slice_rows, stripe)

    stripes = []
    for step in range(narrow_count):
        column = lax.rem(narrow_index + narrow_count - step, narrow_count) * stripe
        part = lax.dynamic_slice(amplitudes, (0, column), (amplitudes.shape[0], stripe))
        stripes.append(shift(part, narrow_count, -step) if step else part)

    tiles = lax.dynamic_slice(tile_block, (wide_index * region_tiles,), (region_tiles,)).astype(jnp.float32)
    columns = (narrow_index * stripe + jnp.arange(stripe, dtype=jnp.int32)) // TILE
    column_blocks = block_of(tiles, columns)

    occ_count = occ_energy.shape[0]
    choosers = (
        occ_pairs.reshape(-1)[:, None] == jnp.arange(occ_count, dtype=jnp.int32)[None, :]
    ).astype(jnp.float32)
    energies = jnp.dot(choosers, occ_energy, precision=lax.Precision.HIGHEST).reshape(occ_pairs.shape[0], 2)
    occupied_sum = (energies[:, 0] + energies[:, 1])[:, None]

    starts = [sum(CHUNKS[:i]) for i in range(len(CHUNKS))]
    sends = [dealt[:, first : first + size] for first, size in zip(starts, CHUNKS)]
    later, _ = lax.optimization_barrier((sends[1:], stripes[1]))
    window, later = gather(stripes, later)
    sends = sends[:1] + later

    def exchange(index, size, after):
        sent = sends[index]
        if after:
            sent, *_ = lax.optimization_barrier((sent, *after))
        arrived = lax.all_to_all(sent, "ta", split_axis=0, concat_axis=0, tiled=True)
        return arrived.reshape(wide_count * size, stripe)

    def shared(arrived, first, size, step):
        per_slice = size // UNIT
        unit = jnp.arange(wide_count * per_slice, dtype=jnp.int32)
        row_tile = ((unit // per_slice) * slice_rows + first + (unit % per_slice) * UNIT) // TILE
        keep = (block_of(tiles, row_tile)[:, None] == column_blocks[None, :]).astype(jnp.float32)
        return product(window, arrived, keep, narrow_count, step)

    def reduced(shares):
        up, down = shares[far], shares[far + 1]
        for hop in range(1, far + 1):
            up = shift(up, narrow_count, 1)
            if hop < far:
                up = (up.astype(jnp.float32) + shares[far - hop].astype(jnp.float32)).astype(jnp.bfloat16)
        for hop in range(1, far):
            down = shift(down, narrow_count, -1)
            if hop < far - 1:
                down = (down.astype(jnp.float32) + shares[far + 1 + hop].astype(jnp.float32)).astype(jnp.bfloat16)
        return [shares[0], up, down]

    group = SPAN
    per_group = group // slice_rows
    far = narrow_count // 2
    places = []
    for first, size in zip(starts, CHUNKS):
        source = jnp.arange(per_group * size, dtype=jnp.int32)
        target = (source // size) * slice_rows + first + source % size
        places.append((target[:, None] == jnp.arange(group, dtype=jnp.int32)[None, :]).astype(jnp.bfloat16))

    arrived = []
    for index, size in enumerate(CHUNKS):
        arrived.append(exchange(index, size, arrived[-1:]))
    pieces = []
    for index, size in enumerate(CHUNKS):
        pieces += reduced(shared(arrived[index], starts[index], size, STEPS[index]))
    return finish(pieces, places, other_terms, occupied_sum, pair_energy[None, :])


def solution(mesh):
    return jax.shard_map(
        shards,
        mesh=mesh,
        in_specs=(P("ka", "ta"), P("ta", "ka"), P("ka", "ta"), P(), P("ka", None), P(), P("ta")),
        out_specs=P("ka", "ta"),
        check_vma=False,
    )
```

```python
import functools

import jax
import jax.numpy as jnp
from jax import lax
from jax.experimental import pallas as pl
from jax.experimental.pallas import tpu as pltpu
from jax.sharding import PartitionSpec as P

TILE = 128
UNIT = 16
COST = pl.CostEstimate(flops=1000, bytes_accessed=1000, transcendentals=0)
CHUNKS = (112, 48)
STEPS = (1792, 768)
SPAN = 1280


def block_of(tiles, index):
    picker = (index[:, None] == jnp.arange(tiles.shape[0], dtype=jnp.int32)[None, :]).astype(jnp.float32)
    return jnp.dot(picker, tiles, precision=lax.Precision.HIGHEST)


def gather(stripes, held):
    count = len(stripes)
    rows, width = stripes[0].shape

    def kernel(*refs):
        window_ref = refs[count + len(held)]
        for slot, stripe in enumerate(refs[:count]):
            window_ref[slot * rows : (slot + 1) * rows, :] = stripe[...]

    vmem, anywhere = pl.BlockSpec(memory_space=pltpu.VMEM), pl.BlockSpec(memory_space=pl.ANY)
    window, *held = pl.pallas_call(
        kernel,
        in_specs=[vmem] * count + [anywhere] * len(held),
        out_specs=[vmem] + [anywhere] * len(held),
        out_shape=[pltpu.VMEM((rows * count, width), stripes[0].dtype)]
        + [pltpu.HBM(h.shape, h.dtype) for h in held],
        input_output_aliases={count + n: 1 + n for n in range(len(held))},
        name="gather_window",
    )(*stripes, *held)
    return window, held


def product_kernel(rings, keep_ref, window_ref, rows_ref, *refs):
    outs, masked_ref = refs[:-1], refs[-1]
    slots = len(outs) // rings
    window = outs[0].shape[0]
    for unit in range(masked_ref.shape[0] // UNIT):
        rows = pl.ds(unit * UNIT, UNIT)
        keep = keep_ref[unit : unit + 1, :].astype(jnp.bfloat16)
        masked_ref[rows, :] = rows_ref[rows, :] * keep
    shares = lax.dot_general(
        window_ref[...], masked_ref[...], (((1,), (1,)), ((), ())), preferred_element_type=jnp.float32
    ).astype(jnp.bfloat16)
    for ring in range(rings):

        @pl.when(pl.program_id(0) // (pl.num_programs(0) // rings) == ring)
        def _():
            for slot in range(slots):
                outs[ring * slots + slot][...] = shares[slot * window : (slot + 1) * window]


def ring_block(rows, width, ring, share):
    return pl.BlockSpec((rows, width), lambda t: (0, jnp.clip(t - ring * share, 0, share - 1)))


def product(window, rows, keep, slots, step, rings, space):
    occ, stripe = window.shape
    count = rows.shape[0]
    return pl.pallas_call(
        functools.partial(product_kernel, rings),
        grid=(count // step,),
        in_specs=[
            pl.BlockSpec((step // UNIT, stripe), lambda t: (t, 0)),
            pl.BlockSpec((occ, stripe), lambda t: (0, 0)),
            pl.BlockSpec((step, stripe), lambda t: (t, 0)),
        ],
        out_specs=[ring_block(occ // slots, step, n // slots, count // step // rings) for n in range(slots * rings)],
        out_shape=[space((occ // slots, count // rings), jnp.bfloat16)] * (slots * rings),
        scratch_shapes=[pltpu.VMEM((step, stripe), jnp.bfloat16)],
        compiler_params=pltpu.CompilerParams(vmem_limit_bytes=24 * 1024 * 1024),
        cost_estimate=COST,
        name="product",
    )(keep, window, rows)


def placed(pieces, place):
    own, up, down = (piece[...].astype(jnp.float32) for piece in pieces)
    share = own + up + down
    high = share.astype(jnp.bfloat16)
    low = (share - high.astype(jnp.float32)).astype(jnp.bfloat16)
    moved = jnp.dot(high, place[...], preferred_element_type=jnp.float32)
    return moved + jnp.dot(low, place[...], preferred_element_type=jnp.float32)


def begin_kernel(own, up, down, place, other_ref, out_ref):
    out_ref[...] = other_ref[...].astype(jnp.float32) + placed((own, up, down), place)


def begin(pieces, place, other_terms, ring, rings):
    window, region = other_terms.shape
    share = region // SPAN // rings
    return pl.pallas_call(
        begin_kernel,
        grid=(share,),
        in_specs=[pl.BlockSpec((window, place.shape[0]), lambda t: (0, t))] * 3
        + [pl.BlockSpec(place.shape, lambda t: (0, 0)), pl.BlockSpec((window, SPAN), lambda t: (0, t + ring * share))],
        out_specs=pl.BlockSpec((window, SPAN), lambda t: (0, t)),
        out_shape=pltpu.VMEM((window, region // rings), jnp.float32),
        compiler_params=pltpu.CompilerParams(vmem_limit_bytes=24 * 1024 * 1024),
        cost_estimate=COST,
        name="begin",
    )(*pieces, place, other_terms)


def finish_kernel(own, up, down, place, *refs):
    residuals, (occ_ref, pair_ref, out_ref) = refs[:-3], refs[-3:]
    last = placed((own, up, down), place)
    for ring, residual in enumerate(residuals):

        @pl.when(pl.program_id(0) // (pl.num_programs(0) // len(residuals)) == ring)
        def _():
            out_ref[...] = (residual[...] + last) / (occ_ref[...] - pair_ref[...])


def finish(pieces, place, residuals, occupied_sum, pair_energy):
    window, region = pieces[0].shape[0], pair_energy.shape[1]
    spans = region // SPAN
    return pl.pallas_call(
        finish_kernel,
        grid=(spans,),
        in_specs=[pl.BlockSpec((window, place.shape[0]), lambda t: (0, t))] * 3
        + [pl.BlockSpec(place.shape, lambda t: (0, 0))]
        + [ring_block(window, SPAN, ring, spans // len(residuals)) for ring in range(len(residuals))]
        + [pl.BlockSpec((window, 1), lambda t: (0, 0)), pl.BlockSpec((1, SPAN), lambda t: (0, t))],
        out_specs=pl.BlockSpec((window, SPAN), lambda t: (0, t)),
        out_shape=jax.ShapeDtypeStruct((window, region), jnp.float32),
        compiler_params=pltpu.CompilerParams(vmem_limit_bytes=24 * 1024 * 1024),
        cost_estimate=COST,
        name="finish",
    )(*pieces, place, *residuals, occupied_sum, pair_energy)


def shift(values, count, step):
    return lax.ppermute(values, "ka", [(i, (i + step) % count) for i in range(count)])


def shards(amplitudes, integrals, other_terms, tile_block, occ_pairs, occ_energy, pair_energy):
    wide_count = lax.axis_size("ta")
    wide_index = lax.axis_index("ta")
    narrow_count = lax.axis_size("ka")
    narrow_index = lax.axis_index("ka")
    region, stripe = integrals.shape
    slice_rows = region // wide_count
    region_tiles = region // TILE
    dealt = integrals.reshape(wide_count, slice_rows, stripe)

    def parts(steps):
        return jnp.stack(
            [
                lax.dynamic_slice(
                    amplitudes,
                    (0, lax.rem(narrow_index + narrow_count + step, narrow_count) * stripe),
                    (amplitudes.shape[0], stripe),
                )
                for step in steps
            ]
        )

    far = narrow_count // 2
    stripes = [None] * narrow_count
    stripes[0] = parts([0])[0]
    rising, falling = parts(range(1, far + 1)), parts(range(-1, -far, -1))
    for hop in range(1, far + 1):
        rising = shift(rising, narrow_count, 1)
        stripes[narrow_count - hop] = rising[0]
        rising = rising[1:]
        if hop < far:
            falling = shift(falling, narrow_count, -1)
            stripes[hop] = falling[0]
            falling = falling[1:]

    tiles = lax.dynamic_slice(tile_block, (wide_index * region_tiles,), (region_tiles,)).astype(jnp.float32)
    columns = (narrow_index * stripe + jnp.arange(stripe, dtype=jnp.int32)) // TILE
    column_blocks = block_of(tiles, columns)

    occ_count = occ_energy.shape[0]
    choosers = (
        occ_pairs.reshape(-1)[:, None] == jnp.arange(occ_count, dtype=jnp.int32)[None, :]
    ).astype(jnp.float32)
    energies = jnp.dot(choosers, occ_energy, precision=lax.Precision.HIGHEST).reshape(occ_pairs.shape[0], 2)
    occupied_sum = (energies[:, 0] + energies[:, 1])[:, None]

    starts = [sum(CHUNKS[:i]) for i in range(len(CHUNKS))]
    sends = [dealt[:, first : first + size] for first, size in zip(starts, CHUNKS)]
    later, _ = lax.optimization_barrier((sends[1:], stripes[1]))
    group = SPAN
    per_group = group // slice_rows
    places = []
    for first, size in zip(starts, CHUNKS):
        source = jnp.arange(per_group * size, dtype=jnp.int32)
        target = (source // size) * slice_rows + first + source % size
        places.append((target[:, None] == jnp.arange(group, dtype=jnp.int32)[None, :]).astype(jnp.bfloat16))
    window, held = gather(stripes, list(later) + places)
    sends, places = sends[:1] + held[: len(later)], held[len(later) :]

    def exchange(index, size, after):
        sent = sends[index]
        if after:
            sent, *_ = lax.optimization_barrier((sent, *after))
        arrived = lax.all_to_all(sent, "ta", split_axis=0, concat_axis=0, tiled=True)
        return arrived.reshape(wide_count * size, stripe)

    def shared(arrived, first, size, step, rings):
        per_slice = size // UNIT
        unit = jnp.arange(wide_count * per_slice, dtype=jnp.int32)
        row_tile = ((unit // per_slice) * slice_rows + first + (unit % per_slice) * UNIT) // TILE
        keep = (block_of(tiles, row_tile)[:, None] == column_blocks[None, :]).astype(jnp.float32)
        space = pltpu.VMEM if first else pltpu.HBM
        return product(window, arrived, keep, narrow_count, step, rings, space)

    def reduced(shares, turn, after):
        long, short = shares[far], shares[(far + turn) % narrow_count]
        for hop in range(1, far + 1):
            if hop == far - 1 and after:
                short, *_ = lax.optimization_barrier((short, *after))
            long = shift(long, narrow_count, turn)
            if hop < far:
                mine = shares[(turn * (far - hop)) % narrow_count]
                long = (long.astype(jnp.float32) + mine.astype(jnp.float32)).astype(jnp.bfloat16)
                short = shift(short, narrow_count, -turn)
            if hop < far - 1:
                mine = shares[(far + turn * (hop + 1)) % narrow_count]
                short = (short.astype(jnp.float32) + mine.astype(jnp.float32)).astype(jnp.bfloat16)
        return [shares[0], long, short]

    arrived = []
    for index, size in enumerate(CHUNKS):
        arrived.append(exchange(index, size, arrived[-1:]))
    shares = [shared(arrived[n], starts[n], CHUNKS[n], STEPS[n], 1) for n in range(len(CHUNKS))]
    pieces = [reduced(shares[0], 1, shares[1][:1]), reduced(shares[1], -1, [])]
    residual = begin(pieces[0], places[0], other_terms, 0, 1)
    return finish(pieces[1], places[1], [residual], occupied_sum, pair_energy[None, :])


def solution(mesh):
    return jax.shard_map(
        shards,
        mesh=mesh,
        in_specs=(P("ka", "ta"), P("ta", "ka"), P("ka", "ta"), P(), P("ka", None), P(), P("ta")),
        out_specs=P("ka", "ta"),
        check_vma=False,
    )
```

```python
import functools

import jax
import jax.numpy as jnp
from jax import lax
from jax.experimental import pallas as pl
from jax.experimental.pallas import tpu as pltpu
from jax.sharding import PartitionSpec as P

TILE = 128
UNIT = 16
COST = pl.CostEstimate(flops=1000, bytes_accessed=1000, transcendentals=0)
CHUNKS = (112, 48)
STEPS = (1792, 768)
SPAN = 1280


def block_of(tiles, index):
    picker = (index[:, None] == jnp.arange(tiles.shape[0], dtype=jnp.int32)[None, :]).astype(jnp.float32)
    return jnp.dot(picker, tiles, precision=lax.Precision.HIGHEST)


def gather(stripes, held):
    count = len(stripes)
    rows, width = stripes[0].shape

    def kernel(*refs):
        window_ref = refs[count + len(held)]
        for slot, stripe in enumerate(refs[:count]):
            window_ref[slot * rows : (slot + 1) * rows, :] = stripe[...]

    vmem, anywhere = pl.BlockSpec(memory_space=pltpu.VMEM), pl.BlockSpec(memory_space=pl.ANY)
    window, *held = pl.pallas_call(
        kernel,
        in_specs=[vmem] * count + [anywhere] * len(held),
        out_specs=[vmem] + [anywhere] * len(held),
        out_shape=[pltpu.VMEM((rows * count, width), stripes[0].dtype)]
        + [pltpu.HBM(h.shape, h.dtype) for h in held],
        input_output_aliases={count + n: 1 + n for n in range(len(held))},
        name="gather_window",
    )(*stripes, *held)
    return window, held


def product_kernel(rings, keep_ref, window_ref, rows_ref, *refs):
    outs, masked_ref = refs[:-1], refs[-1]
    slots = len(outs) // rings
    window = outs[0].shape[0]
    for unit in range(masked_ref.shape[0] // UNIT):
        rows = pl.ds(unit * UNIT, UNIT)
        keep = keep_ref[unit : unit + 1, :].astype(jnp.bfloat16)
        masked_ref[rows, :] = rows_ref[rows, :] * keep
    shares = lax.dot_general(
        window_ref[...], masked_ref[...], (((1,), (1,)), ((), ())), preferred_element_type=jnp.float32
    ).astype(jnp.bfloat16)
    for ring in range(rings):

        @pl.when(pl.program_id(0) // (pl.num_programs(0) // rings) == ring)
        def _():
            for slot in range(slots):
                outs[ring * slots + slot][...] = shares[slot * window : (slot + 1) * window]


def ring_block(rows, width, ring, share):
    return pl.BlockSpec((rows, width), lambda t: (0, jnp.clip(t - ring * share, 0, share - 1)))


def product(window, rows, keep, slots, step, rings, space):
    occ, stripe = window.shape
    count = rows.shape[0]
    return pl.pallas_call(
        functools.partial(product_kernel, rings),
        grid=(count // step,),
        in_specs=[
            pl.BlockSpec((step // UNIT, stripe), lambda t: (t, 0)),
            pl.BlockSpec((occ, stripe), lambda t: (0, 0)),
            pl.BlockSpec((step, stripe), lambda t: (t, 0)),
        ],
        out_specs=[ring_block(occ // slots, step, n // slots, count // step // rings) for n in range(slots * rings)],
        out_shape=[space((occ // slots, count // rings), jnp.bfloat16)] * (slots * rings),
        scratch_shapes=[pltpu.VMEM((step, stripe), jnp.bfloat16)],
        compiler_params=pltpu.CompilerParams(vmem_limit_bytes=24 * 1024 * 1024),
        cost_estimate=COST,
        name="product",
    )(keep, window, rows)


def placed(pieces, place):
    own, up, down = (piece[...].astype(jnp.float32) for piece in pieces)
    share = own + up + down
    high = share.astype(jnp.bfloat16)
    low = (share - high.astype(jnp.float32)).astype(jnp.bfloat16)
    moved = jnp.dot(jnp.concatenate([high, low], axis=0), place[...], preferred_element_type=jnp.float32)
    return moved[: share.shape[0]] + moved[share.shape[0] :]


def begin_kernel(own, up, down, place, other_ref, out_ref):
    out_ref[...] = other_ref[...].astype(jnp.float32) + placed((own, up, down), place)


def begin(pieces, place, other_terms, ring, rings):
    window, region = other_terms.shape
    share = region // SPAN // rings
    return pl.pallas_call(
        begin_kernel,
        grid=(share,),
        in_specs=[pl.BlockSpec((window, place.shape[0]), lambda t: (0, t))] * 3
        + [pl.BlockSpec(place.shape, lambda t: (0, 0)), pl.BlockSpec((window, SPAN), lambda t: (0, t + ring * share))],
        out_specs=pl.BlockSpec((window, SPAN), lambda t: (0, t)),
        out_shape=pltpu.VMEM((window, region // rings), jnp.float32),
        compiler_params=pltpu.CompilerParams(vmem_limit_bytes=24 * 1024 * 1024),
        cost_estimate=COST,
        name="begin",
    )(*pieces, place, other_terms)


def finish_kernel(own, up, down, place, *refs):
    residuals, (occ_ref, pair_ref, out_ref) = refs[:-3], refs[-3:]
    last = placed((own, up, down), place)
    for ring, residual in enumerate(residuals):

        @pl.when(pl.program_id(0) // (pl.num_programs(0) // len(residuals)) == ring)
        def _():
            out_ref[...] = (residual[...] + last) / (occ_ref[...] - pair_ref[...])


def finish(pieces, place, residuals, occupied_sum, pair_energy):
    window, region = pieces[0].shape[0], pair_energy.shape[1]
    spans = region // SPAN
    return pl.pallas_call(
        finish_kernel,
        grid=(spans,),
        in_specs=[pl.BlockSpec((window, place.shape[0]), lambda t: (0, t))] * 3
        + [pl.BlockSpec(place.shape, lambda t: (0, 0))]
        + [ring_block(window, SPAN, ring, spans // len(residuals)) for ring in range(len(residuals))]
        + [pl.BlockSpec((window, 1), lambda t: (0, 0)), pl.BlockSpec((1, SPAN), lambda t: (0, t))],
        out_specs=pl.BlockSpec((window, SPAN), lambda t: (0, t)),
        out_shape=jax.ShapeDtypeStruct((window, region), jnp.float32),
        compiler_params=pltpu.CompilerParams(vmem_limit_bytes=24 * 1024 * 1024),
        cost_estimate=COST,
        name="finish",
    )(*pieces, place, *residuals, occupied_sum, pair_energy)


def shift(values, count, step):
    return lax.ppermute(values, "ka", [(i, (i + step) % count) for i in range(count)])


def shards(amplitudes, integrals, other_terms, tile_block, occ_pairs, occ_energy, pair_energy):
    wide_count = lax.axis_size("ta")
    wide_index = lax.axis_index("ta")
    narrow_count = lax.axis_size("ka")
    narrow_index = lax.axis_index("ka")
    region, stripe = integrals.shape
    slice_rows = region // wide_count
    region_tiles = region // TILE
    dealt = integrals.reshape(wide_count, slice_rows, stripe)

    def parts(steps):
        return jnp.stack(
            [
                lax.dynamic_slice(
                    amplitudes,
                    (0, lax.rem(narrow_index + narrow_count + step, narrow_count) * stripe),
                    (amplitudes.shape[0], stripe),
                )
                for step in steps
            ]
        )

    far = narrow_count // 2
    stripes = [None] * narrow_count
    stripes[0] = parts([0])[0]
    rising, falling = parts(range(1, far + 1)), parts(range(-1, -far, -1))
    for hop in range(1, far + 1):
        rising = shift(rising, narrow_count, 1)
        stripes[narrow_count - hop] = rising[0]
        rising = rising[1:]
        if hop < far:
            falling = shift(falling, narrow_count, -1)
            stripes[hop] = falling[0]
            falling = falling[1:]

    tiles = lax.dynamic_slice(tile_block, (wide_index * region_tiles,), (region_tiles,)).astype(jnp.float32)
    columns = (narrow_index * stripe + jnp.arange(stripe, dtype=jnp.int32)) // TILE
    column_blocks = block_of(tiles, columns)

    occ_count = occ_energy.shape[0]
    choosers = (
        occ_pairs.reshape(-1)[:, None] == jnp.arange(occ_count, dtype=jnp.int32)[None, :]
    ).astype(jnp.float32)
    energies = jnp.dot(choosers, occ_energy, precision=lax.Precision.HIGHEST).reshape(occ_pairs.shape[0], 2)
    occupied_sum = (energies[:, 0] + energies[:, 1])[:, None]

    starts = [sum(CHUNKS[:i]) for i in range(len(CHUNKS))]
    sends = [dealt[:, first : first + size] for first, size in zip(starts, CHUNKS)]
    later, _ = lax.optimization_barrier((sends[1:], stripes[1]))
    group = SPAN
    per_group = group // slice_rows
    places = []
    for first, size in zip(starts, CHUNKS):
        source = jnp.arange(per_group * size, dtype=jnp.int32)
        target = (source // size) * slice_rows + first + source % size
        places.append((target[:, None] == jnp.arange(group, dtype=jnp.int32)[None, :]).astype(jnp.bfloat16))
    window, held = gather(stripes, list(later) + places)
    sends, places = sends[:1] + held[: len(later)], held[len(later) :]

    def exchange(index, size, after):
        sent = sends[index]
        if after:
            sent, *_ = lax.optimization_barrier((sent, *after))
        arrived = lax.all_to_all(sent, "ta", split_axis=0, concat_axis=0, tiled=True)
        return arrived.reshape(wide_count * size, stripe)

    def shared(arrived, first, size, step, rings):
        per_slice = size // UNIT
        unit = jnp.arange(wide_count * per_slice, dtype=jnp.int32)
        row_tile = ((unit // per_slice) * slice_rows + first + (unit % per_slice) * UNIT) // TILE
        keep = (block_of(tiles, row_tile)[:, None] == column_blocks[None, :]).astype(jnp.float32)
        space = pltpu.VMEM if first else pltpu.HBM
        return product(window, arrived, keep, narrow_count, step, rings, space)

    def reduced(shares, turn, after):
        long, short = shares[far], shares[(far + turn) % narrow_count]
        for hop in range(1, far + 1):
            if hop == far - 1 and after:
                short, *_ = lax.optimization_barrier((short, *after))
            long = shift(long, narrow_count, turn)
            if hop < far:
                mine = shares[(turn * (far - hop)) % narrow_count]
                long = (long.astype(jnp.float32) + mine.astype(jnp.float32)).astype(jnp.bfloat16)
                short = shift(short, narrow_count, -turn)
            if hop < far - 1:
                mine = shares[(far + turn * (hop + 1)) % narrow_count]
                short = (short.astype(jnp.float32) + mine.astype(jnp.float32)).astype(jnp.bfloat16)
        return [shares[0], long, short]

    arrived = []
    for index, size in enumerate(CHUNKS):
        arrived.append(exchange(index, size, arrived[-1:]))
    shares = [shared(arrived[n], starts[n], CHUNKS[n], STEPS[n], 1) for n in range(len(CHUNKS))]
    pieces = [reduced(shares[0], 1, shares[1][:1]), reduced(shares[1], -1, [])]
    residual = begin(pieces[0], places[0], other_terms, 0, 1)
    return finish(pieces[1], places[1], [residual], occupied_sum, pair_energy[None, :])


def solution(mesh):
    return jax.shard_map(
        shards,
        mesh=mesh,
        in_specs=(P("ka", "ta"), P("ta", "ka"), P("ka", "ta"), P(), P("ka", None), P(), P("ta")),
        out_specs=P("ka", "ta"),
        check_vma=False,
    )
```

```python
import functools

import jax
import jax.numpy as jnp
from jax import lax
from jax.experimental import pallas as pl
from jax.experimental.pallas import tpu as pltpu
from jax.sharding import PartitionSpec as P

TILE = 128
UNIT = 16
COST = pl.CostEstimate(flops=1000, bytes_accessed=1000, transcendentals=0)
CHUNKS = (112, 48)
STEPS = (1792, 1536)
SPAN = 1280


def block_of(tiles, index):
    picker = (index[:, None] == jnp.arange(tiles.shape[0], dtype=jnp.int32)[None, :]).astype(jnp.float32)
    return jnp.dot(picker, tiles, precision=lax.Precision.HIGHEST)


def gather(stripes, held):
    count = len(stripes)
    rows, width = stripes[0].shape

    def kernel(*refs):
        window_ref = refs[count + len(held)]
        for slot, stripe in enumerate(refs[:count]):
            window_ref[slot * rows : (slot + 1) * rows, :] = stripe[...]

    vmem, anywhere = pl.BlockSpec(memory_space=pltpu.VMEM), pl.BlockSpec(memory_space=pl.ANY)
    window, *held = pl.pallas_call(
        kernel,
        in_specs=[vmem] * count + [anywhere] * len(held),
        out_specs=[vmem] + [anywhere] * len(held),
        out_shape=[pltpu.VMEM((rows * count, width), stripes[0].dtype)]
        + [pltpu.HBM(h.shape, h.dtype) for h in held],
        input_output_aliases={count + n: 1 + n for n in range(len(held))},
        name="gather_window",
    )(*stripes, *held)
    return window, held


def product_kernel(rings, keep_ref, window_ref, rows_ref, *refs):
    outs, masked_ref = refs[:-1], refs[-1]
    slots = len(outs) // rings
    window = outs[0].shape[0]
    for unit in range(masked_ref.shape[0] // UNIT):
        rows = pl.ds(unit * UNIT, UNIT)
        keep = keep_ref[unit : unit + 1, :].astype(jnp.bfloat16)
        masked_ref[rows, :] = rows_ref[rows, :] * keep
    shares = lax.dot_general(
        window_ref[...], masked_ref[...], (((1,), (1,)), ((), ())), preferred_element_type=jnp.float32
    ).astype(jnp.bfloat16)
    for ring in range(rings):

        @pl.when(pl.program_id(0) // (pl.num_programs(0) // rings) == ring)
        def _():
            for slot in range(slots):
                outs[ring * slots + slot][...] = shares[slot * window : (slot + 1) * window]


def ring_block(rows, width, ring, share):
    return pl.BlockSpec((rows, width), lambda t: (0, jnp.clip(t - ring * share, 0, share - 1)))


def product(window, rows, keep, slots, step, rings, space):
    occ, stripe = window.shape
    count = rows.shape[0]
    return pl.pallas_call(
        functools.partial(product_kernel, rings),
        grid=(count // step,),
        in_specs=[
            pl.BlockSpec((step // UNIT, stripe), lambda t: (t, 0)),
            pl.BlockSpec((occ, stripe), lambda t: (0, 0)),
            pl.BlockSpec((step, stripe), lambda t: (t, 0)),
        ],
        out_specs=[ring_block(occ // slots, step, n // slots, count // step // rings) for n in range(slots * rings)],
        out_shape=[space((occ // slots, count // rings), jnp.bfloat16)] * (slots * rings),
        scratch_shapes=[pltpu.VMEM((step, stripe), jnp.bfloat16)],
        compiler_params=pltpu.CompilerParams(vmem_limit_bytes=24 * 1024 * 1024),
        cost_estimate=COST,
        name="product",
    )(keep, window, rows)


def placed(pieces, place):
    own, up, down = (piece[...].astype(jnp.float32) for piece in pieces)
    share = own + up + down
    high = share.astype(jnp.bfloat16)
    low = (share - high.astype(jnp.float32)).astype(jnp.bfloat16)
    moved = jnp.dot(jnp.concatenate([high, low], axis=0), place[...], preferred_element_type=jnp.float32)
    return moved[: share.shape[0]] + moved[share.shape[0] :]


def begin_kernel(own, up, down, place, other_ref, out_ref):
    out_ref[...] = other_ref[...].astype(jnp.float32) + placed((own, up, down), place)


def begin(pieces, place, other_terms, ring, rings):
    window, region = other_terms.shape
    share = region // SPAN // rings
    return pl.pallas_call(
        begin_kernel,
        grid=(share,),
        in_specs=[pl.BlockSpec((window, place.shape[0]), lambda t: (0, t))] * 3
        + [pl.BlockSpec(place.shape, lambda t: (0, 0)), pl.BlockSpec((window, SPAN), lambda t: (0, t + ring * share))],
        out_specs=pl.BlockSpec((window, SPAN), lambda t: (0, t)),
        out_shape=pltpu.VMEM((window, region // rings), jnp.float32),
        compiler_params=pltpu.CompilerParams(vmem_limit_bytes=24 * 1024 * 1024),
        cost_estimate=COST,
        name="begin",
    )(*pieces, place, other_terms)


def finish_kernel(own, up, down, place, *refs):
    residuals, (occ_ref, pair_ref, out_ref) = refs[:-3], refs[-3:]
    last = placed((own, up, down), place)
    for ring, residual in enumerate(residuals):

        @pl.when(pl.program_id(0) // (pl.num_programs(0) // len(residuals)) == ring)
        def _():
            out_ref[...] = (residual[...] + last) / (occ_ref[...] - pair_ref[...])


def finish(pieces, place, residuals, occupied_sum, pair_energy):
    window, region = pieces[0].shape[0], pair_energy.shape[1]
    spans = region // SPAN
    return pl.pallas_call(
        finish_kernel,
        grid=(spans,),
        in_specs=[pl.BlockSpec((window, place.shape[0]), lambda t: (0, t))] * 3
        + [pl.BlockSpec(place.shape, lambda t: (0, 0))]
        + [ring_block(window, SPAN, ring, spans // len(residuals)) for ring in range(len(residuals))]
        + [pl.BlockSpec((window, 1), lambda t: (0, 0)), pl.BlockSpec((1, SPAN), lambda t: (0, t))],
        out_specs=pl.BlockSpec((window, SPAN), lambda t: (0, t)),
        out_shape=jax.ShapeDtypeStruct((window, region), jnp.float32),
        compiler_params=pltpu.CompilerParams(vmem_limit_bytes=24 * 1024 * 1024),
        cost_estimate=COST,
        name="finish",
    )(*pieces, place, *residuals, occupied_sum, pair_energy)


def shift(values, count, step):
    return lax.ppermute(values, "ka", [(i, (i + step) % count) for i in range(count)])


def shards(amplitudes, integrals, other_terms, tile_block, occ_pairs, occ_energy, pair_energy):
    wide_count = lax.axis_size("ta")
    wide_index = lax.axis_index("ta")
    narrow_count = lax.axis_size("ka")
    narrow_index = lax.axis_index("ka")
    region, stripe = integrals.shape
    slice_rows = region // wide_count
    region_tiles = region // TILE
    dealt = integrals.reshape(wide_count, slice_rows, stripe)

    def parts(steps):
        return jnp.stack(
            [
                lax.dynamic_slice(
                    amplitudes,
                    (0, lax.rem(narrow_index + narrow_count + step, narrow_count) * stripe),
                    (amplitudes.shape[0], stripe),
                )
                for step in steps
            ]
        )

    far = narrow_count // 2
    stripes = [None] * narrow_count
    stripes[0] = parts([0])[0]
    rising, falling = parts(range(1, far + 1)), parts(range(-1, -far, -1))
    for hop in range(1, far + 1):
        rising = shift(rising, narrow_count, 1)
        stripes[narrow_count - hop] = rising[0]
        rising = rising[1:]
        if hop < far:
            falling = shift(falling, narrow_count, -1)
            stripes[hop] = falling[0]
            falling = falling[1:]

    tiles = lax.dynamic_slice(tile_block, (wide_index * region_tiles,), (region_tiles,)).astype(jnp.float32)
    columns = (narrow_index * stripe + jnp.arange(stripe, dtype=jnp.int32)) // TILE
    column_blocks = block_of(tiles, columns)

    occ_count = occ_energy.shape[0]
    choosers = (
        occ_pairs.reshape(-1)[:, None] == jnp.arange(occ_count, dtype=jnp.int32)[None, :]
    ).astype(jnp.float32)
    energies = jnp.dot(choosers, occ_energy, precision=lax.Precision.HIGHEST).reshape(occ_pairs.shape[0], 2)
    occupied_sum = (energies[:, 0] + energies[:, 1])[:, None]

    starts = [sum(CHUNKS[:i]) for i in range(len(CHUNKS))]
    sends = [dealt[:, first : first + size] for first, size in zip(starts, CHUNKS)]
    later, _ = lax.optimization_barrier((sends[1:], stripes[1]))
    group = SPAN
    per_group = group // slice_rows
    places = []
    for first, size in zip(starts, CHUNKS):
        source = jnp.arange(per_group * size, dtype=jnp.int32)
        target = (source // size) * slice_rows + first + source % size
        places.append((target[:, None] == jnp.arange(group, dtype=jnp.int32)[None, :]).astype(jnp.bfloat16))
    window, held = gather(stripes, list(later) + places)
    sends, places = sends[:1] + held[: len(later)], held[len(later) :]

    def exchange(index, size, after):
        sent = sends[index]
        if after:
            sent, *_ = lax.optimization_barrier((sent, *after))
        arrived = lax.all_to_all(sent, "ta", split_axis=0, concat_axis=0, tiled=True)
        return arrived.reshape(wide_count * size, stripe)

    def shared(arrived, first, size, step, rings):
        per_slice = size // UNIT
        unit = jnp.arange(wide_count * per_slice, dtype=jnp.int32)
        row_tile = ((unit // per_slice) * slice_rows + first + (unit % per_slice) * UNIT) // TILE
        keep = (block_of(tiles, row_tile)[:, None] == column_blocks[None, :]).astype(jnp.float32)
        space = pltpu.VMEM if first else pltpu.HBM
        return product(window, arrived, keep, narrow_count, step, rings, space)

    def reduced(shares, turn, after):
        long, short = shares[far], shares[(far + turn) % narrow_count]
        for hop in range(1, far + 1):
            if hop == far - 1 and after:
                short, *_ = lax.optimization_barrier((short, *after))
            long = shift(long, narrow_count, turn)
            if hop < far:
                mine = shares[(turn * (far - hop)) % narrow_count]
                long = (long.astype(jnp.float32) + mine.astype(jnp.float32)).astype(jnp.bfloat16)
                short = shift(short, narrow_count, -turn)
            if hop < far - 1:
                mine = shares[(far + turn * (hop + 1)) % narrow_count]
                short = (short.astype(jnp.float32) + mine.astype(jnp.float32)).astype(jnp.bfloat16)
        return [shares[0], long, short]

    arrived = []
    for index, size in enumerate(CHUNKS):
        arrived.append(exchange(index, size, arrived[-1:]))
    shares = [shared(arrived[n], starts[n], CHUNKS[n], STEPS[n], 1) for n in range(len(CHUNKS))]
    pieces = [reduced(shares[0], 1, shares[1][:1]), reduced(shares[1], -1, [])]
    residual = begin(pieces[0], places[0], other_terms, 0, 1)
    return finish(pieces[1], places[1], [residual], occupied_sum, pair_energy[None, :])


def solution(mesh):
    return jax.shard_map(
        shards,
        mesh=mesh,
        in_specs=(P("ka", "ta"), P("ta", "ka"), P("ka", "ta"), P(), P("ka", None), P(), P("ta")),
        out_specs=P("ka", "ta"),
        check_vma=False,
    )
```
